32 devices in a mesh: vp: 8 (over z, x), ch: 4 (over y, core).
Axes of the slice: x: 2, y: 2, z: 4, core: 2. Of those that a mesh axis runs over, the one named last changes fastest.
Arguments:
- chol_a: bfloat16 [640, 4, 6000], P('vp', None, 'ch'), may hold values from -0.078125 to 0.078125
- chol_b: bfloat16 [6000, 8, 640], P('ch', 'vp'), may hold values from -6 to 6
- amplitudes: bfloat16 [640, 8, 640], P('vp'), may hold values from -0.0390625 to 0.0390625
- vir_a: float32 [4], replicated, may hold values from 0.2 to 3
- vir_b: float32 [8], P('vp'), may hold values from 0.2 to 3
- occ_pair: float32 [8], P('ch'), may hold values from -4 to -1
Outputs:
- increment: float32 [4, 8, 8], P(None, 'vp', 'ch')
The draws below stay inside these ranges and needn't reach their ends.
All inputs are finite; a program needn't handle non-finite values.
Results may differ from the reference program's by a relative error of at most 0.0029.
Values may be sent and summed in bfloat16 or wider, within the bound.
No kernel may reach another device: no remote copies, remote signals or barrier semaphores. Data moves between devices by JAX's collectives and lax.ppermute only.
A program may use at most 64 MiB of HBM per device.

```python
import jax
import jax.numpy as jnp
from jax import lax

NV = 640
NCH = 6000
NIJ = 8
NA = 4
NB = 8
N_CH = 4


def block_levels(key, dims, cuts, smallest, top_value):
    gain = 1.0
    for position, blocks in cuts:
        draws = jax.random.uniform(jax.random.fold_in(jax.random.fold_in(key, 6), position), (blocks,), jnp.float32, smallest / len(cuts), top_value / len(cuts))
        gain = gain * jnp.repeat(jnp.exp(draws), dims[position] // blocks).reshape((-1,) + (1,) * (len(dims) - 1 - position))
    return gain


def gaussian(own_key, extent, deviation, bound, pieces=(), kind=jnp.bfloat16):
    drawn = deviation * jax.random.normal(own_key, extent, jnp.float32)
    if pieces:
        drawn = drawn * block_levels(own_key, extent, pieces, -0.22, 0.18)
    return jnp.clip(drawn, -bound, bound).astype(kind)


def setup_inputs(seed: int = 0) -> dict:
    seeds = jax.random.split(jax.random.key(seed), 7)
    chol_a = gaussian(seeds[0], (NV, NA, NCH), NCH ** -0.5, 0.078125, ((0, 8), (2, 4)))
    chol_b = gaussian(seeds[1], (NCH, NB, NV), 1.0, 6.0, ((0, 4), (1, 8)))
    amplitudes = gaussian(seeds[2], (NV, NIJ, NV), (NV * NV // 16) ** -0.5, 0.0390625, ((0, 8),))
    vir_a = jnp.clip(jax.random.uniform(seeds[3], (NA,), jnp.float32, 0.2, 3.0), 0.2, 3.0)
    vir_b = jnp.clip(0.2 + 2.8 * jax.random.uniform(seeds[4], (NB,), jnp.float32) ** block_levels(seeds[4], (NB,), ((0, 8),), -0.2, 0.2), 0.2, 3.0)
    occ_pair = jnp.clip(-4.0 + 3.0 * jax.random.uniform(seeds[5], (NIJ,), jnp.float32) ** block_levels(seeds[5], (NIJ,), ((0, 4),), -0.2, 0.2), -4.0, -1.0)
    return {"chol_a": chol_a, "chol_b": chol_b, "amplitudes": amplitudes, "vir_a": vir_a, "vir_b": vir_b, "occ_pair": occ_pair}


def reference(chol_a, chol_b, amplitudes, vir_a, vir_b, occ_pair):
    slab_width = NCH // N_CH
    left_all = chol_a.reshape(NV * NA, NCH)
    amps_f32 = amplitudes.astype(jnp.float32)

    def ladder_row(b_index):
        running = jnp.zeros((NA, NIJ), jnp.float32)
        for slab_id in range(N_CH):
            left = left_all[:, slab_id * slab_width:(slab_id + 1) * slab_width]
            cholesky_right = lax.dynamic_slice_in_dim(chol_b[slab_id * slab_width:(slab_id + 1) * slab_width], b_index, 1, 1).reshape(slab_width, NV)
            v_rows = jnp.dot(left, cholesky_right, preferred_element_type=jnp.float32).astype(jnp.bfloat16)
            v_rows = lax.optimization_barrier(v_rows).astype(jnp.float32).reshape(NV, NA, NV)
            running = running + jnp.einsum('cad,cid->ai', v_rows, amps_f32, precision=lax.Precision.HIGHEST)
        return running

    ladder = lax.map(ladder_row, jnp.arange(NB, dtype=jnp.int32))
    ladder = jnp.transpose(ladder, (1, 0, 2))
    energy_gap = vir_a[:, None, None] + vir_b[None, :, None] - occ_pair[None, None, :]
    return ladder / energy_gap
```

```python
import functools

import jax
import jax.numpy as jnp
from jax import lax
from jax.experimental import pallas as pl
from jax.experimental.pallas import tpu as pltpu
from jax.sharding import PartitionSpec as P

F32 = jnp.float32
BF16 = jnp.bfloat16
AXES = ("vp", "ch")


def gathered_body(chol_a, chol_b, amplitudes, vir_a, vir_b, occ_pair):
    nch_dev, nb_dev, vir_count = chol_b.shape
    a_count = chol_a.shape[1]
    pair_count = amplitudes.shape[1]
    cholesky_right = chol_b.reshape(nch_dev, nb_dev * vir_count)
    panel_rows = lax.all_gather(chol_a, "vp", axis=0, tiled=True)
    rows_here = panel_rows.shape[0]
    v_rows = jnp.dot(
        panel_rows.reshape(rows_here * a_count, nch_dev),
        cholesky_right,
        preferred_element_type=F32,
    )
    v_all = v_rows.astype(BF16).reshape(rows_here, a_count * nb_dev, vir_count)
    quarter = pair_count // lax.axis_size("ch")
    own_pairs = lax.dynamic_slice_in_dim(amplitudes, lax.axis_index("ch") * quarter, quarter, 1)
    spread = lax.all_gather(own_pairs, "vp", axis=0, tiled=True)
    all_pairs = lax.all_gather(spread, "ch", axis=1, tiled=True)
    ladder = jnp.einsum("cxd,cid->xi", v_all, all_pairs, preferred_element_type=F32)
    ladder = ladder.reshape(a_count, nb_dev, pair_count)
    ladder = lax.psum_scatter(ladder, "ch", scatter_dimension=2, tiled=True)
    energy_gap = vir_a[:, None, None] + vir_b[None, :, None] - occ_pair[None, None, :]
    return ladder / energy_gap


def sends(vp, ch, move):
    pairs = []
    for v in range(vp):
        for c in range(ch):
            target = move(v // 2, v % 2, c // 2, c % 2)
            if target is not None:
                z, x, y, core = target
                pairs.append((v * ch + c, (2 * z + x) * ch + 2 * y + core))
    return pairs


def along_z(table):
    return lambda z, x, y, core: (table[z], x, y, core) if z in table else None


PAIR = along_z({0: 1, 1: 0, 2: 3, 3: 2})
INWARD = along_z({0: 1, 3: 2})
OUTWARD = along_z({1: 0, 2: 3})
MIDDLE = along_z({1: 2, 2: 1})
MIRROR = along_z({0: 3, 1: 2, 2: 1, 3: 0})
FLIP_X = lambda z, x, y, core: (z, 1 - x, y, core)
FLIP_X_INNER = lambda z, x, y, core: (z, 1 - x, y, core) if z in (1, 2) else None
FLIP_Y = lambda z, x, y, core: (z, x, 1 - y, core)
FLIP_CORE = lambda z, x, y, core: (z, x, y, 1 - core)


class Loader:
    def __init__(self, sems):
        self.sems = sems
        self.count = 0
        self.pending = {}

    def start(self, dst, src):
        copy = pltpu.make_async_copy(src, dst, self.sems.at[self.count])
        copy.start()
        self.pending[id(dst)] = (copy, dst)
        self.count += 1
        return dst

    def start_either(self, dst, pred, src_true, src_false):
        sem = self.sems.at[self.count]
        pl.when(pred)(lambda: pltpu.make_async_copy(src_true, dst, sem).start())
        pl.when(jnp.logical_not(pred))(lambda: pltpu.make_async_copy(src_false, dst, sem).start())
        self.pending[id(dst)] = (pltpu.make_async_copy(src_true, dst, sem), dst)
        self.count += 1
        return dst

    def wait(self, dst):
        item = self.pending.pop(id(dst), None)
        if item is not None:
            item[0].wait()


def tile_kernel(slots, mains, nears, names, counts, *refs):
    a_count, ij_count = counts
    n_in = len(names)
    inputs = dict(zip(names, refs[:n_in]))
    out = refs[n_in]
    scratch = list(refs[n_in + 1:])
    sems = scratch.pop()
    total = scratch.pop()
    hi = scratch.pop()
    lo = scratch.pop()
    z = lax.axis_index("vp") // 2
    ch = lax.axis_index("ch")
    inner = jnp.logical_or(z == 1, z == 2)
    load = Loader(sems)
    rights = {}
    held = []
    it = iter(scratch)
    first = True
    for kind, head, tail, pieces in slots:
        item = {"kind": kind}
        for key, src in (("head", head), ("tail", tail)):
            if len(src) == 1:
                item[key] = load.start(next(it), inputs[src[0]])
            else:
                item[key] = load.start_either(next(it), inner, inputs[src[0]], inputs[src[1]])
        if first:
            for name in mains + nears:
                rights[name] = load.start(next(it), inputs[name])
            first = False
        dst = next(it)
        if kind == "own":
            item["amps"] = [load.start(dst, inputs[pieces[0]])]
        else:
            item["amps"] = []
            for m in range(4):
                views = [inputs[p[m][0]] if p[m][1] is None else inputs[p[m][0]].at[p[m][1]] for p in pieces]
                if len(views) == 1:
                    item["amps"].append(load.start(dst.at[m], views[0]))
                else:
                    item["amps"].append(load.start_either(dst.at[m], inner, views[0], views[1]))
        item["amps_ref"] = dst
        held.append(item)
    total[...] = jnp.zeros_like(total)
    quarter = hi.shape[1] // 4
    amp_rows = total.shape[2]

    def contract(stack, targets, item):
        n = len(targets)
        ref = item["amps_ref"]
        acc = None
        for m in range(4):
            if item["kind"] == "own":
                left = stack(pl.ds(quarter * m, quarter))
                right = ref[pl.ds(amp_rows * m, amp_rows), :]
            else:
                j = lax.bitwise_xor(ch, (0, 2, 1, 3)[m])
                left = stack(pl.ds(pl.multiple_of(quarter * j, quarter), quarter))
                right = ref[m]
            part = lax.dot_general(
                left.reshape(n * quarter, left.shape[-1]), right, (((1,), (1,)), ((), ())),
                preferred_element_type=F32,
            )
            acc = part if acc is None else acc + part
        for i, target in enumerate(targets):
            total[target] += acc[i * quarter:(i + 1) * quarter]

    for item in held:
        k_head = item["head"].shape[1]
        own = item["kind"] == "own"
        load.wait(item["head"])
        load.wait(item["tail"])
        for name in mains + nears:
            load.wait(rights[name])
        for dst in item["amps"]:
            load.wait(dst)
        n_main, n_near = len(mains), len(nears)

        def main_tiles(full, low, item=item, k_head=k_head):
            for i, name in enumerate(mains):
                right = rights[name]
                acc = jnp.dot(item["head"][...], right[:k_head, :], preferred_element_type=F32)
                if full:
                    acc += jnp.dot(item["tail"][...], right[k_head:, :], preferred_element_type=F32)
                top = acc.astype(BF16)
                hi[i] = top
                if low:
                    lo[i] = (acc - top.astype(F32)).astype(BF16)

        def near_tiles(item=item):
            for i, name in enumerate(nears):
                acc = jnp.dot(item["tail"][...], rights[name][...], preferred_element_type=F32)
                top = acc.astype(BF16)
                hi[n_main + i] = top
                lo[n_main + i] = (acc - top.astype(F32)).astype(BF16)

        def run(full, low, near, item=item):
            a0, a1 = (0 if full is not None else n_main), (n_main + n_near if near else n_main)
            if full is not None:
                main_tiles(full, low)
            if near:
                near_tiles()
            if a1 > a0:
                contract(lambda rows: hi[a0:a1, rows, :], list(range(a0, a1)), item)
            l0, l1 = (0 if low else n_main), (n_main + n_near if near else n_main)
            if l1 > l0:
                contract(lambda rows: lo[l0:l1, rows, :], list(range(l0, l1)), item)

        has_main = True if mains else None
        if item["kind"] == "first":
            pl.when(inner)(lambda: run(has_main, False, False))
            if mains:
                pl.when(jnp.logical_not(inner))(lambda: run(False, True, False))
        elif own:
            if mains:
                run(True, False, False)
            if nears:
                pl.when(inner)(lambda: run(None, False, True))
        else:
            pl.when(inner)(lambda: run(has_main, False, bool(nears)))
            if mains:
                pl.when(jnp.logical_not(inner))(lambda: run(False, True, False))

    n = total.shape[0]
    shape = (quarter, amp_rows)
    same_c = (
        lax.broadcasted_iota(jnp.int32, shape, 0) // a_count
        == lax.broadcasted_iota(jnp.int32, shape, 1) // ij_count
    )
    picked = jnp.where(same_c[None], total[...], 0.0)
    summed = picked.reshape(n, quarter // a_count, a_count, amp_rows).sum(1).reshape(n * a_count, amp_rows)
    fold = lax.broadcasted_iota(jnp.int32, (amp_rows, ij_count), 0) % ij_count
    fold = (fold == lax.broadcasted_iota(jnp.int32, (amp_rows, ij_count), 1)).astype(F32)
    out[...] = jnp.dot(summed, fold, precision=lax.Precision.HIGHEST, preferred_element_type=F32)


def tile_call(arrays, slots, mains, nears, counts, name):
    a_count, ij_count = counts
    names = []

    def use(n):
        if n not in names:
            names.append(n)

    scratch = []
    first = True
    for kind, head, tail, pieces in slots:
        for src in (head, tail):
            for n in src:
                use(n)
            scratch.append(pltpu.VMEM(arrays[src[0]].shape, BF16))
        if first:
            for n in mains + nears:
                use(n)
                scratch.append(pltpu.VMEM(arrays[n].shape, BF16))
            first = False
        if kind == "own":
            use(pieces[0])
            shape = arrays[pieces[0]].shape
            scratch.append(pltpu.VMEM(shape, BF16))
            quarter_rows = shape[0] // 4
        else:
            for p in pieces:
                for n, _ in p:
                    use(n)
            n, index = pieces[0][0]
            shape = arrays[n].shape if index is None else arrays[n].shape[1:]
            scratch.append(pltpu.VMEM((4,) + shape, BF16))
            quarter_rows = shape[0]
    rows = arrays[slots[0][1][0]].shape[0]
    width = arrays[(mains + nears)[0]].shape[1]
    n = len(mains) + len(nears)
    scratch += [
        pltpu.VMEM((n, rows, width), BF16),
        pltpu.VMEM((n, rows, width), BF16),
        pltpu.VMEM((n, rows // 4, quarter_rows), F32),
        pltpu.SemaphoreType.DMA((8 * len(slots) + n,)),
    ]
    out = pl.pallas_call(
        functools.partial(tile_kernel, slots, mains, nears, tuple(names), counts),
        out_shape=jax.ShapeDtypeStruct((n * a_count, ij_count), F32),
        in_specs=[pl.BlockSpec(memory_space=pl.ANY)] * len(names),
        out_specs=pl.BlockSpec(memory_space=pltpu.VMEM),
        scratch_shapes=scratch,
        name=name,
    )(*[arrays[k] for k in names])
    return out.reshape(n, a_count, ij_count)


def line_body(vp, ch, chol_a, chol_b, amplitudes, vir_a, vir_b, occ_pair):
    nch_dev, _, width = chol_b.shape
    c_dev, a_count, _ = chol_a.shape
    ij_count = amplitudes.shape[1]
    counts = (a_count, ij_count)
    k_head = nch_dev * 2 // 3 // 128 * 128 + (128 if nch_dev * 2 // 3 % 128 > 64 else 0)
    where = lax.axis_index("ch")

    def go(name, value, move):
        with jax.named_scope(name):
            return lax.ppermute(value, AXES, sends(vp, ch, move))

    arr = {}
    rights = chol_b.reshape(nch_dev, width)
    arr["b"] = rights
    arr["bx"] = go("bx", rights, FLIP_X)
    q_rows = c_dev // 4
    own_quarter = lax.dynamic_slice_in_dim(amplitudes, where * q_rows, q_rows, 0).reshape(q_rows * ij_count, width)
    arr["t"] = amplitudes.reshape(c_dev * ij_count, width)
    ta = go("ta", own_quarter, PAIR)
    tb = go("tb", own_quarter, MIRROR)
    left = chol_a.reshape(c_dev * a_count, nch_dev)
    head, tail = left[:, :k_head], left[:, k_head:]
    arr["h"], arr["l"] = head, tail
    arr["h1"] = go("p1", head, PAIR)
    h2 = go("p2", head, MIDDLE)
    tc = go("tc", tb, PAIR)
    arr["t1"] = jnp.stack([ta, tb])
    arr["ty1"] = go("ty1", arr["t1"], FLIP_Y)
    arr["tk1"] = go("tk1", jnp.concatenate([arr["t1"], arr["ty1"]]), FLIP_CORE)
    h3 = go("p3", arr["h1"], MIDDLE)
    arr["near"] = go("br", rights[k_head:], INWARD)
    arr["l1"] = go("p1b", tail, INWARD)
    arr["h2i"], arr["h2o"] = h2, go("p4", h2, OUTWARD)
    arr["l2"] = go("p2b", tail, MIDDLE)
    arr["t2"] = tc
    arr["ty2"] = go("ty2", tc, FLIP_Y)
    arr["tk2"] = go("tk2", jnp.stack([tc, arr["ty2"]]), FLIP_CORE)
    arr["h3i"], arr["h3o"] = h3, go("p5", h3, OUTWARD)
    arr["l3"] = go("p3b", arr["l1"], MIDDLE)
    arr["nearx"] = go("brx", arr["near"], FLIP_X_INNER)

    p_a = (("t1", 0), ("ty1", 0), ("tk1", 0), ("tk1", 2))
    p_b = (("t1", 1), ("ty1", 1), ("tk1", 1), ("tk1", 3))
    p_c = (("t2", None), ("ty2", None), ("tk2", 0), ("tk2", 1))
    own = ("own", ("h",), ("l",), ("t",))
    slot1 = ("first", ("h1",), ("l1",), (p_a,))
    slot2 = ("far", ("h2i", "h2o"), ("l2",), (p_b, p_c))
    slot3 = ("far", ("h3i", "h3o"), ("l3",), (p_c, p_b))
    k0 = tile_call(arr, (own,), ("b",), (), counts, "k0")
    k1 = tile_call(arr, (own,), ("bx",), (), counts, "k1")
    k2 = tile_call(arr, (slot1, slot2), ("b", "bx"), (), counts, "k2")
    k3 = tile_call(arr, (slot3,), ("b", "bx"), ("near", "nearx"), counts, "k3")
    k4 = tile_call(arr, (own, slot2), (), ("near", "nearx"), counts, "k4")
    kept = jnp.concatenate([k0, k1]) + k2 + k3[:2]
    near = k3[2:] + k4
    kept = kept + go("rz", near, OUTWARD)
    ladder = kept[0] + go("rx", kept[1], FLIP_X)
    ladder = ladder + go("ry", ladder, FLIP_Y)
    ladder = ladder + go("rk", ladder, FLIP_CORE)
    pairs = ij_count // ch
    ladder = lax.dynamic_slice_in_dim(ladder, where * pairs, pairs, 1)[:, None, :]
    energy_gap = vir_a[:, None, None] + vir_b[None, :, None] - occ_pair[None, None, :]
    return ladder / energy_gap


def solution(mesh):
    vp, ch = mesh.shape["vp"], mesh.shape["ch"]
    on_line = vp == 8 and ch == 4

    def body(*args):
        if on_line:
            return line_body(vp, ch, *args)
        return gathered_body(*args)

    return jax.shard_map(
        body,
        mesh=mesh,
        in_specs=(
            P("vp", None, "ch"),
            P("ch", "vp", None),
            P("vp", None, None),
            P(),
            P("vp"),
            P("ch"),
        ),
        out_specs=P(None, "vp", "ch"),
        check_vma=False,
    )
```
